32 devices in a mesh: tm: 2 (over core), height: 16 (over z, y, x).
Axes of the slice: x: 2, y: 2, z: 4, core: 2. Of those that a mesh axis runs over, the one named last changes fastest.
Arguments:
- clean_latents: bfloat16 [8, 64, 16, 3072], P('tm', 'height'), may hold values from -6 to 6
- gaussian_noise: bfloat16 [8, 64, 16, 3072], P('tm', 'height'), may hold values from -6 to 6
- text_states: bfloat16 [256, 3072], replicated, may hold values from -6 to 6
- queries: bfloat16 [8, 64, 16, 1536], P('tm', 'height'), may hold values from -40 to 40
- key_states: bfloat16 [8, 64, 16, 1536], P('tm', 'height'), may hold values from -8 to 8
- cotangent: bfloat16 [8, 64, 16, 1536], P('tm', 'height'), may hold values from -240 to 240
- text_keys: bfloat16 [256, 1536], replicated, may hold values from -6 to 6
- window_radii: int32 [12, 3], replicated, may hold values from 0 to 1
- timestep: int32 [1], replicated, may hold values from 200 to 799
- sketch_seed: int32 [1], replicated, may hold values from 0 to 65535
- down_image: bfloat16 [3072, 16], replicated, may hold values from -0.109375 to 0.109375
- up_image: bfloat16 [16, 1536], replicated, may hold values from -1.5 to 1.5
- down_text: bfloat16 [3072, 16], replicated, may hold values from -0.109375 to 0.109375
- up_text: bfloat16 [16, 1536], replicated, may hold values from -1.5 to 1.5
Outputs:
- value_grad: bfloat16 [8, 64, 16, 1536], P('tm', 'height')
- grad_sketch: float32 [16384], replicated
The draws below stay inside these ranges and needn't reach their ends.
All inputs are finite; a program needn't handle non-finite values.
Results may differ from the reference program's by a relative error of at most 0.0075.
Values may be sent and summed in bfloat16 or wider, within the bound.
No kernel may reach another device: no remote copies, remote signals or barrier semaphores. Data moves between devices by JAX's collectives and lax.ppermute only.
A program may use at most 128 MiB of HBM per device.

```python
import jax
import jax.numpy as jnp
from jax import lax

D = 3072
HDIM = 128
TXT = 256
HEADS = 12
RANK = 16
SKETCH = 16384
FT = 4
HR = 4
TW = 8
W = 16
HD = 1536
NF = 8
NR = 64
TOKENS = 8192
PARAMS = 147456
N_TM = 2
N_HEIGHT = 16


def drawn_pair(key):
    query_key = jax.random.fold_in(key, 11)
    key_key = jax.random.fold_in(key, 12)
    shape = (NF, NR, W, HD)
    base_keys = jnp.clip(jax.random.normal(key_key, shape, jnp.float32), -4.0, 4.0)
    base_queries = jnp.clip(jax.random.normal(query_key, shape, jnp.float32), -4.0, 4.0)
    return (base_queries, base_keys)


def draw_queries(key, part):
    return drawn_pair(key)[0].astype(jnp.bfloat16)


def draw_key_states(key, part):
    return drawn_pair(key)[1].astype(jnp.bfloat16)


def with_ends(drawn, stream_key, least, top_value):
    place = [jax.random.randint(jax.random.fold_in(stream_key, axis), (), 0, length) for axis, length in enumerate(drawn.shape)]
    widest = drawn.shape.index(max(drawn.shape))
    neighbour = place[:widest] + [(place[widest] + 1) % drawn.shape[widest]] + place[widest + 1:]
    return drawn.at[tuple(place)].set(least).at[tuple(neighbour)].set(top_value)


def level_of(own_key, extent, split, low, top_value):
    factor_of = 1.0
    for dim, shards_of in split:
        draws = jax.random.uniform(jax.random.fold_in(jax.random.fold_in(own_key, 6), dim), (shards_of,), jnp.float32, low / len(split), top_value / len(split))
        factor_of = factor_of * jnp.repeat(jnp.exp(draws), extent[dim] // shards_of).reshape((-1,) + (1,) * (len(extent) - 1 - dim))
    return factor_of


def noise(rng, extent, deviation, limit, cuts=(), kind=jnp.bfloat16):
    array = deviation * jax.random.normal(rng, extent, jnp.float32)
    if cuts:
        array = array * level_of(rng, extent, cuts, -0.22, 0.18)
    return jnp.clip(array, -limit, limit).astype(kind)


def setup_inputs(seed: int = 0) -> dict:
    splits = jax.random.split(jax.random.key(seed), 15)
    clean_latents = noise(splits[0], (NF, NR, W, D), 1.0, 6.0, ((0, 2), (1, 16)))
    gaussian_noise = noise(splits[1], (NF, NR, W, D), 1.0, 6.0, ((0, 2), (1, 16)))
    text_states = noise(splits[2], (TXT, D), 1.0, 6.0)
    queries = draw_queries(jax.random.fold_in(splits[14], 71), 0)
    key_states = draw_key_states(jax.random.fold_in(splits[14], 71), 0)
    cotangent = noise(splits[5], (NF, NR, W, HD), 40.0, 240.0, ((0, 2), (1, 16)))
    text_keys = noise(splits[6], (TXT, HD), 1.0, 6.0)
    window_radii = with_ends(jax.random.randint(splits[7], (HEADS, 3), 0, 2), jax.random.fold_in(splits[7], 1), 0, 1).astype(jnp.int32)
    timestep = jax.random.randint(splits[8], (1,), 200, 800).astype(jnp.int32)
    sketch_seed = jax.random.randint(splits[9], (1,), 0, 65536).astype(jnp.int32)
    down_image = noise(splits[10], (D, RANK), D ** -0.5, 0.109375)
    up_image = noise(splits[11], (RANK, HD), RANK ** -0.5, 1.5)
    down_text = noise(splits[12], (D, RANK), D ** -0.5, 0.109375)
    up_text = noise(splits[13], (RANK, HD), RANK ** -0.5, 1.5)
    return {"clean_latents": clean_latents, "gaussian_noise": gaussian_noise, "text_states": text_states, "queries": queries, "key_states": key_states, "cotangent": cotangent, "text_keys": text_keys, "window_radii": window_radii, "timestep": timestep, "sketch_seed": sketch_seed, "down_image": down_image, "up_image": up_image, "down_text": down_text, "up_text": up_text}


def tile_rows(block, width):
    frame_count, row_count, col_count = block.shape[0], block.shape[1], block.shape[2]
    rest = block.shape[3:]
    col_tiles = col_count // width
    shaped = block.reshape((frame_count, row_count, col_tiles, width) + rest)
    order = (2, 0, 1, 3) + tuple(range(4, 4 + len(rest)))
    return jnp.transpose(shaped, order).reshape((col_tiles, frame_count * row_count * width) + rest)


def region_rows(padded, width):
    col_count = padded.shape[2] - 2 * width
    views = [tile_rows(padded[:, :, shift_col * width:shift_col * width + col_count], width) for shift_col in range(3)]
    return jnp.concatenate(views, axis=1)


def window_mask(radius, frame_tile, row_tile, frame_tiles, row_tiles, col_tiles, frame_count, row_count, width):
    region = 27 * frame_count * row_count * width
    position = jnp.arange(region, dtype=jnp.int32)
    col_step = position // (9 * frame_count * row_count * width) - 1
    frame_step = (position // (3 * row_count * width)) % (3 * frame_count) // frame_count - 1
    row_step = (position // width) % (3 * row_count) // row_count - 1
    inside = (jnp.abs(frame_step) <= radius[0]) & (jnp.abs(row_step) <= radius[1]) & (jnp.abs(col_step) <= radius[2])
    inside = inside & (frame_tile + frame_step >= 0) & (frame_tile + frame_step < frame_tiles)
    inside = inside & (row_tile + row_step >= 0) & (row_tile + row_step < row_tiles)
    col_index = jnp.arange(col_tiles, dtype=jnp.int32)[:, None]
    return inside[None, :] & (col_index + col_step[None, :] >= 0) & (col_index + col_step[None, :] < col_tiles)


def forward_head(query_head, key_region, text_head, cot_head, allowed, score_scale):
    image_scores = jnp.einsum('cqd,cld->cql', query_head.astype(jnp.float32), key_region.astype(jnp.float32)) * score_scale
    image_scores = jnp.where(allowed[:, None, :], image_scores, -jnp.inf)
    text_scores = jnp.einsum('cqd,td->cqt', query_head.astype(jnp.float32), text_head.astype(jnp.float32)) * score_scale
    row_max = jnp.maximum(jnp.max(image_scores, axis=-1), jnp.max(text_scores, axis=-1))
    total = jnp.sum(jnp.exp(image_scores - row_max[..., None]), axis=-1) + jnp.sum(jnp.exp(text_scores - row_max[..., None]), axis=-1)
    log_total = row_max + jnp.log(total)
    text_probs = jnp.exp(text_scores - log_total[..., None]).astype(jnp.bfloat16)
    text_part = jnp.einsum('cqt,cqd->td', text_probs.astype(jnp.float32), cot_head.astype(jnp.float32))
    return log_total, text_part


def backward_head(query_region, cot_region, key_head, log_region, allowed, score_scale):
    scores = jnp.einsum('cld,cqd->clq', query_region.astype(jnp.float32), key_head.astype(jnp.float32)) * score_scale
    probs = jnp.where(allowed[:, :, None], jnp.exp(scores - log_region[..., None]), 0.0).astype(jnp.bfloat16)
    return jnp.einsum('clq,cld->cqd', probs.astype(jnp.float32), cot_region.astype(jnp.float32))


def sketch_signs(seed_value, rows, width):
    row_part = jnp.arange(rows, dtype=jnp.int32)[:, None] * width
    position = row_part + jnp.arange(width, dtype=jnp.int32)[None, :]
    mixed_bits = position * 1103515245 + seed_value * 12345 + 1013904223
    mixed_bits = mixed_bits ^ (mixed_bits >> 16)
    mixed_bits = mixed_bits * 73244475
    mixed_bits = mixed_bits ^ (mixed_bits >> 16)
    return (1 - 2 * ((mixed_bits >> 7) & 1)).astype(jnp.float32)


def count_sketch(pieces, seed_value, width, sketch_scale):
    flat = jnp.concatenate([piece.reshape(-1) for piece in pieces]).reshape(-1, width)
    signed = flat * sketch_signs(seed_value, flat.shape[0], width)
    return jnp.sum(signed, axis=0) * sketch_scale


def mat_product(left, right):
    return jnp.dot(left.astype(jnp.float32), right.astype(jnp.float32), precision=lax.Precision.HIGHEST)


def reference(clean_latents, gaussian_noise, text_states, queries, key_states, cotangent, text_keys, window_radii, timestep, sketch_seed, down_image, up_image, down_text, up_text):
    col_tiles = W // TW
    score_scale = HDIM ** -0.5
    pad_spec = ((FT, FT), (HR, HR), (TW, TW), (0, 0))
    key_pad = jnp.pad(key_states, pad_spec)
    zero_start = jnp.zeros((), jnp.int32)
    block_ids = jnp.arange(N_TM * N_HEIGHT, dtype=jnp.int32)
    head_ids = jnp.arange(HEADS, dtype=jnp.int32)

    def block_start(block_index):
        frame_tile = (block_index // N_HEIGHT).astype(jnp.int32)
        row_tile = (block_index % N_HEIGHT).astype(jnp.int32)
        return frame_tile, row_tile, ((frame_tile * FT).astype(jnp.int32), (row_tile * HR).astype(jnp.int32), zero_start, zero_start)

    def split_heads(block, axis):
        moved = jnp.moveaxis(block, axis, -1)
        shaped = moved.reshape(moved.shape[:-1] + (HEADS, HDIM))
        return jnp.moveaxis(shaped, -2, 0)

    def forward_block(carry, block_index):
        frame_tile, row_tile, start = block_start(block_index)
        own_q = split_heads(tile_rows(lax.dynamic_slice(queries, start, (FT, HR, W, HD)), TW), 2)
        own_c = split_heads(tile_rows(lax.dynamic_slice(cotangent, start, (FT, HR, W, HD)), TW), 2)
        near_k = split_heads(region_rows(lax.dynamic_slice(key_pad, start, (3 * FT, 3 * HR, W + 2 * TW, HD)), TW), 2)
        text_h = split_heads(text_keys, 1)

        def per_head(head_index, query_head, key_region, text_head, cot_head):
            allowed = window_mask(window_radii[head_index], frame_tile, row_tile, N_TM, N_HEIGHT, col_tiles, FT, HR, TW)
            return forward_head(query_head, key_region, text_head, cot_head, allowed, score_scale)

        log_total, text_part = jax.vmap(per_head)(head_ids, own_q, near_k, text_h, own_c)
        text_part = jnp.transpose(text_part, (1, 0, 2)).reshape(TXT, HD)
        return carry + text_part, log_total

    text_value, log_blocks = lax.scan(forward_block, jnp.zeros((TXT, HD), jnp.float32), block_ids)
    log_tokens = log_blocks.reshape(N_TM, N_HEIGHT, HEADS, col_tiles, FT, HR, TW)
    log_tokens = jnp.transpose(log_tokens, (0, 4, 1, 5, 3, 6, 2)).reshape(NF, NR, W, HEADS)
    query_pad = jnp.pad(queries, pad_spec)
    cot_pad = jnp.pad(cotangent, pad_spec)
    log_pad = jnp.pad(log_tokens, pad_spec)

    def backward_block(block_index):
        frame_tile, row_tile, start = block_start(block_index)
        own_k = split_heads(tile_rows(lax.dynamic_slice(key_states, start, (FT, HR, W, HD)), TW), 2)
        near_q = split_heads(region_rows(lax.dynamic_slice(query_pad, start, (3 * FT, 3 * HR, W + 2 * TW, HD)), TW), 2)
        near_c = split_heads(region_rows(lax.dynamic_slice(cot_pad, start, (3 * FT, 3 * HR, W + 2 * TW, HD)), TW), 2)
        log_region = jnp.moveaxis(region_rows(lax.dynamic_slice(log_pad, start, (3 * FT, 3 * HR, W + 2 * TW, HEADS)), TW), 2, 0)

        def per_head(head_index, query_region, cot_region, key_head, head_log):
            allowed = window_mask(window_radii[head_index], frame_tile, row_tile, N_TM, N_HEIGHT, col_tiles, FT, HR, TW)
            return backward_head(query_region, cot_region, key_head, head_log, allowed, score_scale)

        return jax.vmap(per_head)(head_ids, near_q, near_c, own_k, log_region)

    grads = lax.map(backward_block, block_ids)
    grads = grads.reshape(N_TM, N_HEIGHT, HEADS, col_tiles, FT, HR, TW, HDIM)
    value_f32 = jnp.transpose(grads, (0, 4, 1, 5, 3, 6, 2, 7)).reshape(NF, NR, W, HD)
    value_grad = value_f32.astype(jnp.bfloat16)

    noise_level = timestep[0].astype(jnp.float32) / 1000.0
    mixed = ((1.0 - noise_level) * clean_latents.astype(jnp.float32) + noise_level * gaussian_noise.astype(jnp.float32)).astype(jnp.bfloat16)
    mixed = mixed.reshape(TOKENS, D)
    flat_value = value_grad.reshape(TOKENS, HD)
    hidden = mat_product(mixed, down_image).astype(jnp.bfloat16)
    grad_up = mat_product(hidden.T, flat_value)
    backward_low = mat_product(flat_value, up_image.T).astype(jnp.bfloat16)
    grad_down = mat_product(mixed.T, backward_low)
    text_hidden = mat_product(text_states, down_text)
    text_up_grad = mat_product(text_hidden.T, text_value)
    text_back = mat_product(text_value, up_text.T)
    text_down_grad = mat_product(text_states.T, text_back)
    sketch_scale = (TOKENS * (PARAMS // SKETCH)) ** -0.5
    grad_sketch = count_sketch((grad_down, grad_up, text_down_grad, text_up_grad), sketch_seed[0], SKETCH, sketch_scale)
    return value_grad, grad_sketch
```

```python
import functools

import jax
import jax.numpy as jnp
import numpy as np
from jax import lax
from jax.experimental import pallas as pl
from jax.experimental.pallas import tpu as pltpu
from jax.sharding import PartitionSpec as P

SKETCH = 16384
TW = 8
LANES = 128
NEGATIVE = -1e30
VMEM_LIMIT = 56 * 1024 * 1024
ADAPTIVE = False


def even_partner(index, count):
    other = index ^ 1
    return other if other < count else None


def odd_partner(index, count):
    other = index + 1 if index % 2 else index - 1
    return other if 0 <= other < count else None


def frame_source(kind, index, count):
    sibling = even_partner(index, count)
    if kind == "self":
        return index
    if kind == "sib":
        return sibling
    if kind == "oself":
        return odd_partner(index, count)
    return None if sibling is None else odd_partner(sibling, count)


def row_source(kind, index, count):
    if kind == "own":
        return index
    return even_partner(index, count) if kind == "even" else odd_partner(index, count)


def slot_pairs(slot, frames, rows):
    pairs = []
    for a in range(frames):
        for i in range(rows):
            f = frame_source(slot[0], a, frames)
            r = row_source(slot[1], i, rows)
            if f is not None and r is not None:
                pairs.append((f * rows + r, a * rows + i))
    return pairs


def is_mine(slot):
    return slot[0] in ("self", "osib")


def call(kernel, outs, ins, grid, scratch=(), prefetch=0, name=None, flops=0, nbytes=0):
    return pl.pallas_call(
        kernel,
        out_shape=[o[0] for o in outs],
        grid_spec=pltpu.PrefetchScalarGridSpec(
            num_scalar_prefetch=prefetch,
            grid=grid,
            in_specs=ins,
            out_specs=[o[1] for o in outs],
            scratch_shapes=list(scratch),
        ),
        compiler_params=pltpu.CompilerParams(vmem_limit_bytes=VMEM_LIMIT),
        cost_estimate=pl.CostEstimate(flops=flops, bytes_accessed=nbytes, transcendentals=0),
        name=name,
    )


def struct(shape, dtype):
    return jax.ShapeDtypeStruct(shape, dtype)


def whole(shape):
    return pl.BlockSpec(shape, lambda *_: (0,) * len(shape))


def pack(sources, sel, counts, name):
    tokens, width = sources[0].shape
    half = sel.shape[0] // 2
    n_src = len(sources)

    def kernel(sel_ref, *refs):
        srcs, outs = refs[:n_src], refs[n_src:]
        for part, out in enumerate(outs):
            for number, src in enumerate(srcs):
                for j in range(counts):
                    at = pl.multiple_of(sel_ref[part * half + j] * LANES, LANES)
                    out[number * counts + j] = src[:, pl.ds(at, LANES)]

    shape = (n_src * counts, tokens, LANES)
    out = (struct(shape, jnp.bfloat16), whole(shape))
    return call(
        kernel,
        [out, out],
        [whole((tokens, width))] * n_src,
        (1,),
        prefetch=1,
        name=name,
        nbytes=4 * n_src * counts * tokens * LANES,
    )(sel, *sources)


def attention(
    sel, radii, exist, mine, recv, halo, text_keys, first, count, slots, half, scale, col_count, name
):
    tokens = mine.shape[1]
    text = text_keys.shape[0]
    n_slot = len(slots)
    queries = ("self", "sib")
    factor = scale * float(np.log2(np.e))
    local = [s for s in slots if s in (("self", "own"), ("sib", "own"))]
    far = [s for s in slots if s not in local]

    def kernel(sel_ref, radii_ref, exist_ref, *refs):
        q_refs = dict(zip(queries, refs[0:2]))
        c_refs = dict(zip(queries, refs[2:4]))
        k_refs = dict(zip(slots, refs[4 : 4 + n_slot]))
        text_ref = refs[4 + n_slot]
        outs = refs[5 + n_slot : 6 + 2 * n_slot]
        dv_refs = dict(zip(slots, outs[:n_slot]))
        dt_ref = outs[n_slot]
        s_scr, p_scr, m_scr, l_scr, acc_scr = refs[6 + 2 * n_slot :]
        head = sel_ref[first + pl.program_id(0)]
        reach = [radii_ref[3 * head + axis] for axis in range(3)]
        shape = (col_count, tokens)
        key_tile = lax.broadcasted_iota(jnp.int32, shape, 0) // TW
        query_tile = lax.broadcasted_iota(jnp.int32, shape, 1) % col_count // TW
        bias = jnp.where(jnp.abs(key_tile - query_tile) <= reach[2], 0.0, NEGATIVE)

        acc = {}
        for index, slot in enumerate(far):
            acc[slot] = acc_scr.at[index]
            acc_scr[index] = jnp.zeros((tokens, LANES), jnp.float32)
        for slot in local:
            acc[slot] = dv_refs[slot].at[0]
            dv_refs[slot][0] = jnp.zeros((tokens, LANES), jnp.float32)

        for query in queries:
            other = "sib" if query == "self" else "self"
            outside = "o" + query

            def condition(slot):
                ok = None
                if slot[0] == other:
                    ok = reach[0] >= 1
                elif slot[0] == outside:
                    ok = (reach[0] >= 1) & (exist_ref[2 + (outside == "osib")] > 0)
                if slot[1] != "own":
                    row = (reach[1] >= 1) & (exist_ref[int(slot[1] == "odd")] > 0)
                    ok = row if ok is None else ok & row
                return ok

            def guarded(slot, body):
                ok = condition(slot)
                if ok is None:
                    body()
                else:
                    pl.when(ok)(body)

            seen = [s for s in slots if s[0] in (query, other, outside)]
            q = q_refs[query][0]

            def product(keys):
                return lax.dot_general(
                    keys, q, (((1,), (1,)), ((), ())), preferred_element_type=jnp.float32
                )

            s_text = product(text_ref[...])
            s_scr[n_slot, :text] = s_text
            m_scr[...] = jnp.max(s_text, axis=0, keepdims=True)
            for slot in seen:

                def scores(slot=slot):
                    s = product(k_refs[slot][0])
                    s = s.reshape(tokens // col_count, col_count, tokens) + bias[None]
                    s = s.reshape(tokens, tokens)
                    s_scr[slots.index(slot), :tokens] = s
                    m_scr[...] = jnp.maximum(m_scr[...], jnp.max(s, axis=0, keepdims=True))

                guarded(slot, scores)

            top = m_scr[...]

            def weights(index, rows):
                p = jnp.exp2((s_scr[index, :rows] - top) * factor)
                p_scr[index, :rows] = p.astype(jnp.bfloat16)
                return jnp.sum(p, axis=0, keepdims=True)

            l_scr[...] = weights(n_slot, text)
            for slot in seen:

                def exponentials(slot=slot):
                    l_scr[...] += weights(slots.index(slot), tokens)

                guarded(slot, exponentials)

            inverse = jnp.broadcast_to(1.0 / l_scr[...], (8, tokens)).T[:, :1]
            cot = (c_refs[query][0].astype(jnp.float32) * inverse).astype(jnp.bfloat16)
            d_text = jnp.dot(p_scr[n_slot, :text], cot, preferred_element_type=jnp.float32)
            if query == queries[0]:
                dt_ref[0] = d_text
            else:
                dt_ref[0] += d_text
            for slot in seen:

                def gradients(slot=slot):
                    acc[slot][...] += jnp.dot(
                        p_scr[slots.index(slot), :tokens], cot, preferred_element_type=jnp.float32
                    )

                guarded(slot, gradients)

        for index, slot in enumerate(far):
            dv_refs[slot][0] = acc_scr[index].astype(jnp.bfloat16)

    block = (1, tokens, LANES)

    def at(base):
        return pl.BlockSpec(block, lambda g, *_: (base + g, 0, 0))

    ins = [at(first), at(first), at(half + first), at(half + first)]
    operands = [mine, recv, mine, recv]
    for slot in slots:
        if slot in local:
            ins.append(at(2 * half + first))
            operands.append(mine if slot[0] == "self" else recv)
        else:
            ins.append(at(first if slot[1] == "own" else 0))
            operands.append(halo[slot])
    ins.append(pl.BlockSpec((text, LANES), lambda g, sel, *_: (0, sel[first + g])))
    operands.append(text_keys)
    outs = [
        (
            struct((count, tokens, LANES), jnp.float32 if s in local else jnp.bfloat16),
            pl.BlockSpec(block, lambda g, *_: (g, 0, 0)),
        )
        for s in slots
    ]
    outs.append(
        (
            struct((count, text, LANES), jnp.float32),
            pl.BlockSpec((1, text, LANES), lambda g, *_: (g, 0, 0)),
        )
    )
    most = max(tokens, text)
    scratch = [
        pltpu.VMEM((n_slot + 1, most, tokens), jnp.float32),
        pltpu.VMEM((n_slot + 1, most, tokens), jnp.bfloat16),
        pltpu.VMEM((1, tokens), jnp.float32),
        pltpu.VMEM((1, tokens), jnp.float32),
        pltpu.VMEM((max(len(far), 1), tokens, LANES), jnp.float32),
    ]
    results = call(
        kernel,
        outs,
        ins,
        (count,),
        scratch,
        prefetch=3,
        name=name,
        flops=count * (n_slot + 1) * 8 * tokens * tokens * LANES,
        nbytes=count * (2 * n_slot + 6) * tokens * LANES * 2,
    )(sel, radii, exist, *operands)
    return dict(zip(slots, results[:n_slot])), results[n_slot]


def sign_block(seed_value, rows):
    position = lax.broadcasted_iota(jnp.int32, (rows, LANES), 0) * LANES
    position = position + lax.broadcasted_iota(jnp.int32, (rows, LANES), 1)
    bits = position * 1103515245 + seed_value * 12345 + 1013904223
    bits = bits ^ (bits >> 16)
    bits = bits * 73244475
    bits = bits ^ (bits >> 16)
    return (1 - 2 * ((bits >> 7) & 1)).astype(jnp.float32)


def prepare(clean, noise, text_states, down_t, down_text_t, level, seed, total_rows, name):
    tokens, width = clean.shape
    text = text_states.shape[0]
    rank = down_t.shape[0]
    rep = LANES // rank
    chunk = 4 * LANES
    steps = width // chunk
    rows = chunk // rep

    def kernel(level_ref, seed_ref, c_ref, n_ref, t_ref, d_ref, dt_ref, *refs):
        mix_ref, txt_ref, hid_ref, thid_ref, sign_ref, a_scr, b_scr, h_scr = refs
        step = pl.program_id(0)
        keep = level_ref[0]
        mixed = (1.0 - keep) * c_ref[...].astype(jnp.float32) + keep * n_ref[...].astype(jnp.float32)
        mixed = mixed.astype(jnp.bfloat16)
        nt = (((1,), (1,)), ((), ()))
        hid = lax.dot_general(d_ref[...], mixed, nt, preferred_element_type=jnp.float32)
        thid = lax.dot_general(dt_ref[...], t_ref[...], nt, preferred_element_type=jnp.float32)

        @pl.when(step == 0)
        def _():
            h_scr[...] = hid
            thid_ref[...] = thid
            sign_ref[...] = sign_block(seed_ref[0], total_rows)

        @pl.when(step > 0)
        def _():
            h_scr[...] += hid
            thid_ref[...] += thid

        hid_ref[...] = h_scr[...].astype(jnp.bfloat16)
        for value, scr, out, count in (
            (mixed, a_scr, mix_ref, tokens),
            (t_ref[...], b_scr, txt_ref, text),
        ):
            wide = value.astype(jnp.float32)
            for b in range(count // LANES):
                scr[b] = wide[b * LANES : (b + 1) * LANES].T
                for k in range(rep):
                    part = scr.at[b][pl.ds(k, rows, stride=rep), :]
                    at = k * count + b * LANES
                    out[:, at : at + LANES] = part.astype(jnp.bfloat16)

    col = lambda n: pl.BlockSpec((n, chunk), lambda g, *_: (0, g))
    row = lambda n: pl.BlockSpec((rows, n), lambda g, *_: (g, 0))
    outs = [
        (struct((width // rep, rep * tokens), jnp.bfloat16), row(rep * tokens)),
        (struct((width // rep, rep * text), jnp.bfloat16), row(rep * text)),
        (struct((rank, tokens), jnp.bfloat16), whole((rank, tokens))),
        (struct((rank, text), jnp.float32), whole((rank, text))),
        (struct((total_rows, LANES), jnp.float32), whole((total_rows, LANES))),
    ]
    scratch = [
        pltpu.VMEM((tokens // LANES, chunk, LANES), jnp.float32),
        pltpu.VMEM((text // LANES, chunk, LANES), jnp.float32),
        pltpu.VMEM((rank, tokens), jnp.float32),
    ]
    return call(
        kernel,
        outs,
        [col(tokens), col(tokens), col(text), col(rank), col(rank)],
        (steps,),
        scratch,
        prefetch=2,
        name=name,
        flops=40 * tokens * width * rank,
        nbytes=12 * tokens * width,
    )(level, seed, clean, noise, text_states, down_t, down_text_t)


def spread_rows(value, rep, rank):
    group = lax.broadcasted_iota(jnp.int32, value.shape, 1) // rank
    return jnp.concatenate([jnp.where(group == k, value, 0.0) for k in range(rep)], axis=0)


def signed_sum(grad_ref, sign_ref, sketch_rows):
    total = None
    for m in range(grad_ref.shape[0] // sketch_rows):
        at = pl.ds(m * sketch_rows, sketch_rows)
        term = grad_ref[at, :] * sign_ref[at, :]
        total = term if total is None else total + term
    return total


def text_sketch(sel, parts, up_text, text_hidden_t, regrouped, signs, offsets, sketch_rows, name):
    rank, width = up_text.shape
    rep = LANES // rank
    text = text_hidden_t.shape[1]
    heads = width // LANES
    n_part = len(parts)
    highest = lax.Precision.HIGHEST
    down_rows = regrouped.shape[0]

    def kernel(sel_ref, *refs):
        tv_refs = refs[:n_part]
        up_ref, hid_ref, reg_ref, sign_ref, out_ref, grad_scr = refs[n_part:]
        grad_scr[...] = jnp.zeros_like(grad_scr)
        back = jnp.zeros((text, LANES), jnp.float32)
        j = 0
        for tv_ref in tv_refs:
            for index in range(tv_ref.shape[0]):
                tv = tv_ref[index]
                head = sel_ref[j]
                at = pl.multiple_of(head * LANES, LANES)
                up = jnp.concatenate([up_ref[:, pl.ds(at, LANES)].astype(jnp.float32)] * rep, axis=0)
                back += lax.dot_general(
                    tv, up, (((1,), (1,)), ((), ())), precision=highest,
                    preferred_element_type=jnp.float32,
                )
                grad_scr[pl.ds(offsets[1] + head, rank, stride=heads), :] = jnp.dot(
                    hid_ref[...], tv, precision=highest, preferred_element_type=jnp.float32
                )
                j += 1
        rest = spread_rows(back, rep, rank)
        down = jnp.zeros((down_rows, LANES), jnp.float32)
        for _ in range(3):
            piece = rest.astype(jnp.bfloat16)
            rest = rest - piece.astype(jnp.float32)
            down += jnp.dot(reg_ref[...], piece, preferred_element_type=jnp.float32)
        grad_scr[pl.ds(offsets[0], down_rows), :] = down
        out_ref[...] = signed_sum(grad_scr, sign_ref, sketch_rows)

    operands = [*parts, up_text, text_hidden_t, regrouped, signs]
    out_shape = (sketch_rows, LANES)
    return call(
        kernel,
        [(struct(out_shape, jnp.float32), whole(out_shape))],
        [whole(x.shape) for x in operands],
        (1,),
        [pltpu.VMEM(signs.shape, jnp.float32)],
        prefetch=1,
        name=name,
        flops=6 * text * down_rows * rep * LANES,
        nbytes=sum(x.size * x.dtype.itemsize for x in operands),
    )(sel, *operands)[0]


def finish(sel, pieces, up_image, hidden_t, regrouped, signs, text_part, offsets, sketch_scale, name):
    rank, width = up_image.shape
    rep = LANES // rank
    tokens = hidden_t.shape[1]
    heads = width // LANES
    half = heads // 2
    down_rows = regrouped.shape[0]
    flat = [(part, first, array) for part in (0, 1) for array, first in pieces[part]]
    n_piece = len(flat)
    sketch_rows = text_part.shape[0]

    def kernel(sel_ref, *refs):
        piece_refs = refs[:n_piece]
        up_ref, hid_ref, reg_ref, sign_ref, text_ref = refs[n_piece : n_piece + 5]
        value_ref, out_ref, grad_scr = refs[n_piece + 5 :]
        grad_scr[...] = jnp.zeros_like(grad_scr)
        back = jnp.zeros((tokens, LANES), jnp.float32)
        for part in (0, 1):
            for j in range(half):
                value = None
                for (owner, first, array), ref in zip(flat, piece_refs):
                    if owner == part and first <= j < first + array.shape[0]:
                        term = ref[j - first].astype(jnp.float32)
                        value = term if value is None else value + term
                value = value.astype(jnp.bfloat16)
                head = sel_ref[part * half + j]
                at = pl.multiple_of(head * LANES, LANES)
                value_ref[:, pl.ds(at, LANES)] = value
                up = jnp.concatenate([up_ref[:, pl.ds(at, LANES)]] * rep, axis=0)
                back += lax.dot_general(
                    value, up, (((1,), (1,)), ((), ())), preferred_element_type=jnp.float32
                )
                grad_scr[pl.ds(offsets[1] + head, rank, stride=heads), :] = jnp.dot(
                    hid_ref[...], value, preferred_element_type=jnp.float32
                )
        back = back.astype(jnp.bfloat16).astype(jnp.float32)
        spread = spread_rows(back, rep, rank).astype(jnp.bfloat16)
        grad_scr[pl.ds(offsets[0], down_rows), :] = jnp.dot(
            reg_ref[...], spread, preferred_element_type=jnp.float32
        )
        total = signed_sum(grad_scr, sign_ref, sketch_rows) + text_ref[...]
        out_ref[...] = total * sketch_scale

    operands = [x for _, _, x in flat] + [up_image, hidden_t, regrouped, signs, text_part]
    outs = [
        (struct((tokens, width), jnp.bfloat16), whole((tokens, width))),
        (struct((sketch_rows, LANES), jnp.float32), whole((sketch_rows, LANES))),
    ]
    return call(
        kernel,
        outs,
        [whole(x.shape) for x in operands],
        (1,),
        [pltpu.VMEM(signs.shape, jnp.float32)],
        prefetch=1,
        name=name,
        flops=4 * tokens * down_rows * rep * LANES,
        nbytes=sum(x.size * x.dtype.itemsize for x in operands),
    )(sel, *operands)


def axis_sum(value, axis):
    count = lax.axis_size(axis)
    if count & (count - 1):
        return lax.psum(value, axis)
    stride = 1
    while stride < count:
        masks = [stride]
        if stride * 4 <= count:
            masks = [stride, 2 * stride, 3 * stride]
        received = [
            lax.ppermute(value, axis, [(i, i ^ mask) for i in range(count)]) for mask in masks
        ]
        for other in received:
            value = value + other
        stride *= 2 * ((len(masks) + 1) // 2)
    return value


def per_device(
    clean_latents,
    gaussian_noise,
    text_states,
    queries,
    key_states,
    cotangent,
    text_keys,
    window_radii,
    timestep,
    sketch_seed,
    down_image,
    up_image,
    down_text,
    up_text,
):
    frame_count, row_count, col_count, value_width = queries.shape
    head_count = window_radii.shape[0]
    tokens = frame_count * row_count * col_count
    half = head_count // 2
    frames, rows = lax.axis_size("tm"), lax.axis_size("height")
    axes = ("tm", "height")
    score_scale = (value_width // head_count) ** (-0.5)
    frame_tile, row_tile = lax.axis_index("tm"), lax.axis_index("height")
    side = frame_tile % 2

    rank, model_width = up_image.shape[0], down_image.shape[0]
    down_rows, up_rows = rank * model_width // LANES, rank * value_width // LANES
    total_rows = 2 * (down_rows + up_rows)
    sketch_rows = SKETCH // LANES
    sketch_scale = (tokens * frames * rows * (total_rows // sketch_rows)) ** (-0.5)

    need = (window_radii[:, 1] > 0).astype(jnp.int32)
    ids = jnp.arange(head_count, dtype=jnp.int32)
    ahead = (need[None, :] > need[:, None]) | (
        (need[None, :] == need[:, None]) & (ids[None, :] < ids[:, None])
    )
    place = jnp.sum(ahead.astype(jnp.int32), axis=1)
    slot_ids = jnp.arange(half, dtype=jnp.int32)
    wanted = jnp.concatenate([2 * slot_ids + side, 2 * slot_ids + 1 - side])
    sel = jnp.sum(jnp.where(place[None, :] == wanted[:, None], ids[None, :], 0), axis=1)
    sel = sel.astype(jnp.int32)
    radii = window_radii.reshape(-1)

    def present(source, count, index):
        table = np.array([source(i, count) is not None for i in range(count)], np.int32)
        return jnp.sum(jnp.where(jnp.arange(count) == index, table, 0)).astype(jnp.int32)

    exist = jnp.stack(
        [
            present(even_partner, rows, row_tile),
            present(odd_partner, rows, row_tile),
            present(functools.partial(frame_source, "oself"), frames, frame_tile),
            present(functools.partial(frame_source, "osib"), frames, frame_tile),
        ]
    )

    all_slots = [
        (f, r) for r in ("own", "even", "odd") for f in ("self", "sib", "oself", "osib")
    ]
    pairs = {s: slot_pairs(s, frames, rows) for s in all_slots}
    all_slots = [s for s in all_slots if pairs[s]]
    own_slots = [s for s in all_slots if s[1] == "own"]
    row_slots = [s for s in all_slots if s[1] != "own"]
    outer_slots = [s for s in own_slots if s[0] in ("oself", "osib")]

    flat = lambda x: x.reshape(tokens, x.shape[-1])
    q2, k2, c2 = flat(queries), flat(key_states), flat(cotangent)
    level = timestep.astype(jnp.float32) / 1000.0

    def give_back(slot, array):
        return lax.ppermute(array, axes, [(b, a) for a, b in pairs[slot]])

    def branch(reach_rows):
        halo = {}
        if reach_rows:
            near = pack([k2], sel, reach_rows, "pack_keys")
            for slot in row_slots:
                halo[slot] = lax.ppermute(near[0 if is_mine(slot) else 1], axes, pairs[slot])
        mine, other = pack([q2, c2, k2], sel, half, "pack_all")
        recv = lax.ppermute(other, axes, pairs[("sib", "own")])
        for slot in outer_slots:
            keys = (mine if is_mine(slot) else other)[2 * half :]
            halo[slot] = lax.ppermute(keys, axes, pairs[slot])
        regrouped, text_regrouped, hidden_t, text_hidden_t, signs = prepare(
            flat(clean_latents),
            flat(gaussian_noise),
            text_states,
            down_image.T,
            down_text.T,
            level,
            sketch_seed,
            total_rows,
            "prepare",
        )
        pieces = {0: [], 1: []}
        text_parts = []

        def attend(first, count, slots, name):
            grads, text_value = attention(
                sel, radii, exist, mine, recv, halo, text_keys, first, count, slots, half,
                score_scale, col_count, name,
            )
            text_parts.append(text_value)
            for slot in slots:
                array = grads[slot]
                if slot != ("self", "own"):
                    array = give_back(slot, array)
                pieces[0 if is_mine(slot) else 1].append((array, first))

        if reach_rows:
            attend(0, reach_rows, all_slots, "attend_rows")
        if reach_rows < half:
            attend(reach_rows, half - reach_rows, own_slots, "attend_own")
        text_part = text_sketch(
            sel, text_parts, up_text, text_hidden_t, text_regrouped, signs,
            (down_rows + up_rows, 2 * down_rows + up_rows), sketch_rows, "text_sketch",
        )
        return finish(
            sel, pieces, up_image, hidden_t, regrouped, signs, text_part,
            (0, down_rows), sketch_scale, "finish",
        )

    if ADAPTIVE:
        count = (jnp.sum(need) + 1) // 2
        value, sketch = lax.switch(
            count, [functools.partial(branch, n) for n in range(half + 1)]
        )
    else:
        value, sketch = branch(half)
    sketch = axis_sum(axis_sum(sketch, "tm"), "height")
    return value.reshape(queries.shape), sketch.reshape(SKETCH)


def solution(mesh):
    tokens_spec = P("tm", "height", None, None)
    return jax.shard_map(
        per_device,
        mesh=mesh,
        in_specs=(
            tokens_spec,
            tokens_spec,
            P(),
            tokens_spec,
            tokens_spec,
            tokens_spec,
            P(),
            P(),
            P(),
            P(),
            P(),
            P(),
            P(),
            P(),
        ),
        out_specs=(tokens_spec, P()),
        check_vma=False,
    )
```

```python
import functools

import jax
import jax.numpy as jnp
import numpy as np
from jax import lax
from jax.experimental import pallas as pl
from jax.experimental.pallas import tpu as pltpu
from jax.sharding import PartitionSpec as P

SKETCH = 16384
TW = 8
LANES = 128
NEGATIVE = -1e30
VMEM_LIMIT = 56 * 1024 * 1024
BRANCHES = (2, 3, 4, 6)


def even_partner(index, count):
    other = index ^ 1
    return other if other < count else None


def odd_partner(index, count):
    other = index + 1 if index % 2 else index - 1
    return other if 0 <= other < count else None


def frame_source(kind, index, count):
    sibling = even_partner(index, count)
    if kind == "self":
        return index
    if kind == "sib":
        return sibling
    if kind == "oself":
        return odd_partner(index, count)
    return None if sibling is None else odd_partner(sibling, count)


def row_source(kind, index, count):
    if kind == "own":
        return index
    return even_partner(index, count) if kind == "even" else odd_partner(index, count)


def slot_pairs(slot, frames, rows):
    pairs = []
    for a in range(frames):
        for i in range(rows):
            f = frame_source(slot[0], a, frames)
            r = row_source(slot[1], i, rows)
            if f is not None and r is not None:
                pairs.append((f * rows + r, a * rows + i))
    return pairs


def is_mine(slot):
    return slot[0] in ("self", "osib")


def call(kernel, outs, ins, grid, scratch=(), prefetch=0, name=None, flops=0, nbytes=0):
    return pl.pallas_call(
        kernel,
        out_shape=[o[0] for o in outs],
        grid_spec=pltpu.PrefetchScalarGridSpec(
            num_scalar_prefetch=prefetch,
            grid=grid,
            in_specs=ins,
            out_specs=[o[1] for o in outs],
            scratch_shapes=list(scratch),
        ),
        compiler_params=pltpu.CompilerParams(vmem_limit_bytes=VMEM_LIMIT),
        cost_estimate=pl.CostEstimate(flops=flops, bytes_accessed=nbytes, transcendentals=0),
        name=name,
    )


def struct(shape, dtype):
    return jax.ShapeDtypeStruct(shape, dtype)


def whole(shape):
    return pl.BlockSpec(shape, lambda *_: (0,) * len(shape))


def pack(sources, sel, counts, name):
    tokens, width = sources[0].shape
    half = sel.shape[0] // 2
    n_src = len(sources)

    def kernel(sel_ref, *refs):
        srcs, outs = refs[:n_src], refs[n_src:]
        for part, out in enumerate(outs):
            for number, src in enumerate(srcs):

                def one(j, carry, src=src, out=out, number=number, part=part):
                    at = pl.multiple_of(sel_ref[part * half + j] * LANES, LANES)
                    out[number * counts + j] = src[:, pl.ds(at, LANES)]
                    return carry

                lax.fori_loop(0, counts, one, 0)

    shape = (n_src * counts, tokens, LANES)
    out = (struct(shape, jnp.bfloat16), whole(shape))
    return call(
        kernel,
        [out, out],
        [whole((tokens, width))] * n_src,
        (1,),
        prefetch=1,
        name=name,
        nbytes=4 * n_src * counts * tokens * LANES,
    )(sel, *sources)


def attention(
    sel, radii, exist, mine, recv, halo, text_keys, first, count, slots, half, scale, col_count, name
):
    tokens = mine.shape[1]
    text = text_keys.shape[0]
    n_slot = len(slots)
    order = ("oself", "self", "sib", "osib")
    groups = [f for f in order if any(s[0] == f for s in slots)]
    row_kinds = [r for r in ("own", "even", "odd") if any(s[1] == r for s in slots)]
    n_group, n_row = len(groups), len(row_kinds)
    base = groups.index("self")
    image = n_row * tokens
    stack = image + text
    factor = scale * float(np.log2(np.e))
    local = (("self", "own"), ("sib", "own"))

    def kernel(sel_ref, radii_ref, exist_ref, *refs):
        q_refs, c_refs = refs[0:2], refs[2:4]
        k_refs = dict(zip(slots, refs[4 : 4 + n_slot]))
        text_ref = refs[4 + n_slot]
        outs = refs[5 + n_slot : 6 + 2 * n_slot]
        q_scr, c_scr, k_scr, s_scr, p_scr, d_scr, bias_scr = refs[6 + 2 * n_slot :]
        head = sel_ref[first + pl.program_id(0)]
        reach = [radii_ref[3 * head + axis] for axis in range(3)]
        key_tile = lax.broadcasted_iota(jnp.int32, (col_count, tokens), 0) // TW
        query_tile = lax.broadcasted_iota(jnp.int32, (col_count, tokens), 1) % col_count // TW
        columns = jnp.where(jnp.abs(key_tile - query_tile) <= reach[2], 0.0, NEGATIVE)

        for f in range(2):
            q_scr[f] = q_refs[f][0]
            c_scr[f] = c_refs[f][0]
        for g, frame in enumerate(groups):
            d_scr[g] = jnp.zeros((stack, LANES), jnp.float32)
            k_scr[g, image:] = text_ref[...]
            for r, kind in enumerate(row_kinds):
                k_scr[g, r * tokens : (r + 1) * tokens] = k_refs[(frame, kind)][0]
                ok = None
                if frame in ("oself", "osib"):
                    ok = exist_ref[2 + (frame == "osib")] > 0
                if kind != "own":
                    row = (reach[1] >= 1) & (exist_ref[int(kind == "odd")] > 0)
                    ok = row if ok is None else ok & row
                shift = 0.0 if ok is None else jnp.where(ok, 0.0, NEGATIVE)
                bias_scr[g, r] = columns + shift

        def query(f, carry):
            own = base + f
            near = (reach[0] >= 1).astype(jnp.int32)
            low = jnp.maximum(own - near, 0)
            high = jnp.minimum(own + near, n_group - 1) + 1
            q = q_scr[f]

            def scores(g, top):
                s = lax.dot_general(
                    k_scr[g], q, (((1,), (1,)), ((), ())), preferred_element_type=jnp.float32
                )
                pixels = s[:image].reshape(n_row, tokens // col_count, col_count, tokens)
                pixels = (pixels + bias_scr[g][:, None]).reshape(image, tokens)
                words = s[image:] + jnp.where(g == own, 0.0, NEGATIVE)
                s_scr[g, :image] = pixels
                s_scr[g, image:] = words
                top = jnp.maximum(top, jnp.max(pixels, axis=0, keepdims=True))
                return jnp.maximum(top, jnp.max(words, axis=0, keepdims=True))

            top = lax.fori_loop(low, high, scores, jnp.full((1, tokens), 2 * NEGATIVE, jnp.float32))

            def weights(g, total):
                p = jnp.exp2((s_scr[g] - top) * factor)
                p_scr[g] = p.astype(jnp.bfloat16)
                return total + jnp.sum(p, axis=0, keepdims=True)

            total = lax.fori_loop(low, high, weights, jnp.zeros((1, tokens), jnp.float32))
            inverse = jnp.broadcast_to(1.0 / total, (8, tokens)).T[:, :1]
            cot = (c_scr[f].astype(jnp.float32) * inverse).astype(jnp.bfloat16)

            def gradients(g, carry):
                d_scr[g] += jnp.dot(p_scr[g], cot, preferred_element_type=jnp.float32)
                return carry

            return lax.fori_loop(low, high, gradients, carry)

        lax.fori_loop(0, 2, query, 0)
        words = None
        for g, frame in enumerate(groups):
            term = d_scr[g, image:]
            words = term if words is None else words + term
            for r, kind in enumerate(row_kinds):
                out = outs[slots.index((frame, kind))]
                out[0] = d_scr[g, r * tokens : (r + 1) * tokens].astype(out.dtype)
        outs[n_slot][0] = words

    block = (1, tokens, LANES)

    def at(start):
        return pl.BlockSpec(block, lambda g, *_: (start + g, 0, 0))

    ins = [at(first), at(first), at(half + first), at(half + first)]
    operands = [mine, recv, mine, recv]
    for slot in slots:
        if slot in local:
            ins.append(at(2 * half + first))
            operands.append(mine if slot[0] == "self" else recv)
        else:
            ins.append(at(first if slot[1] == "own" else 0))
            operands.append(halo[slot])
    ins.append(pl.BlockSpec((text, LANES), lambda g, sel, *_: (0, sel[first + g])))
    operands.append(text_keys)
    outs = [
        (
            struct((count, tokens, LANES), jnp.float32 if s in local else jnp.bfloat16),
            pl.BlockSpec(block, lambda g, *_: (g, 0, 0)),
        )
        for s in slots
    ]
    outs.append(
        (
            struct((count, text, LANES), jnp.float32),
            pl.BlockSpec((1, text, LANES), lambda g, *_: (g, 0, 0)),
        )
    )
    scratch = [
        pltpu.VMEM((2, tokens, LANES), jnp.bfloat16),
        pltpu.VMEM((2, tokens, LANES), jnp.bfloat16),
        pltpu.VMEM((n_group, stack, LANES), jnp.bfloat16),
        pltpu.VMEM((n_group, stack, tokens), jnp.float32),
        pltpu.VMEM((n_group, stack, tokens), jnp.bfloat16),
        pltpu.VMEM((n_group, stack, LANES), jnp.float32),
        pltpu.VMEM((n_group, n_row, col_count, tokens), jnp.float32),
    ]
    results = call(
        kernel,
        outs,
        ins,
        (count,),
        scratch,
        prefetch=3,
        name=name,
        flops=count * (n_slot + 1) * 8 * tokens * tokens * LANES,
        nbytes=count * (2 * n_slot + 6) * tokens * LANES * 2,
    )(sel, radii, exist, *operands)
    return dict(zip(slots, results[:n_slot])), results[n_slot]


def sign_block(seed_value, rows):
    position = lax.broadcasted_iota(jnp.int32, (rows, LANES), 0) * LANES
    position = position + lax.broadcasted_iota(jnp.int32, (rows, LANES), 1)
    bits = position * 1103515245 + seed_value * 12345 + 1013904223
    bits = bits ^ (bits >> 16)
    bits = bits * 73244475
    bits = bits ^ (bits >> 16)
    return (1 - 2 * ((bits >> 7) & 1)).astype(jnp.float32)


def prepare(clean, noise, text_states, down_t, down_text_t, level, seed, total_rows, name):
    tokens, width = clean.shape
    text = text_states.shape[0]
    rank = down_t.shape[0]
    rep = LANES // rank
    chunk = 4 * LANES
    steps = width // chunk
    rows = chunk // rep

    def kernel(level_ref, seed_ref, c_ref, n_ref, t_ref, d_ref, dt_ref, *refs):
        mix_ref, txt_ref, hid_ref, thid_ref, sign_ref, a_scr, b_scr, h_scr = refs
        step = pl.program_id(0)
        keep = level_ref[0]
        mixed = (1.0 - keep) * c_ref[...].astype(jnp.float32) + keep * n_ref[...].astype(jnp.float32)
        mixed = mixed.astype(jnp.bfloat16)
        nt = (((1,), (1,)), ((), ()))
        hid = lax.dot_general(d_ref[...], mixed, nt, preferred_element_type=jnp.float32)
        thid = lax.dot_general(dt_ref[...], t_ref[...], nt, preferred_element_type=jnp.float32)

        @pl.when(step == 0)
        def _():
            h_scr[...] = hid
            thid_ref[...] = thid
            sign_ref[...] = sign_block(seed_ref[0], total_rows)

        @pl.when(step > 0)
        def _():
            h_scr[...] += hid
            thid_ref[...] += thid

        hid_ref[...] = h_scr[...].astype(jnp.bfloat16)
        for value, scr, out, count in (
            (mixed, a_scr, mix_ref, tokens),
            (t_ref[...], b_scr, txt_ref, text),
        ):
            wide = value.astype(jnp.float32)
            for b in range(count // LANES):
                scr[b] = wide[b * LANES : (b + 1) * LANES].T
                for k in range(rep):
                    part = scr.at[b][pl.ds(k, rows, stride=rep), :]
                    at = k * count + b * LANES
                    out[:, at : at + LANES] = part.astype(jnp.bfloat16)

    col = lambda n: pl.BlockSpec((n, chunk), lambda g, *_: (0, g))
    row = lambda n: pl.BlockSpec((rows, n), lambda g, *_: (g, 0))
    outs = [
        (struct((width // rep, rep * tokens), jnp.bfloat16), row(rep * tokens)),
        (struct((width // rep, rep * text), jnp.bfloat16), row(rep * text)),
        (struct((rank, tokens), jnp.bfloat16), whole((rank, tokens))),
        (struct((rank, text), jnp.float32), whole((rank, text))),
        (struct((total_rows, LANES), jnp.float32), whole((total_rows, LANES))),
    ]
    scratch = [
        pltpu.VMEM((tokens // LANES, chunk, LANES), jnp.float32),
        pltpu.VMEM((text // LANES, chunk, LANES), jnp.float32),
        pltpu.VMEM((rank, tokens), jnp.float32),
    ]
    return call(
        kernel,
        outs,
        [col(tokens), col(tokens), col(text), col(rank), col(rank)],
        (steps,),
        scratch,
        prefetch=2,
        name=name,
        flops=40 * tokens * width * rank,
        nbytes=12 * tokens * width,
    )(level, seed, clean, noise, text_states, down_t, down_text_t)


def split(value):
    terms = []
    for _ in range(3):
        terms.append(value.astype(jnp.bfloat16))
        value = value - terms[-1].astype(jnp.float32)
    return terms


def spread_rows(value, rep, rank):
    group = lax.broadcasted_iota(jnp.int32, value.shape, 1) // rank
    return jnp.concatenate([jnp.where(group == k, value, 0.0) for k in range(rep)], axis=0)


def signed_sum(grad_ref, sign_ref, sketch_rows):
    total = None
    for m in range(grad_ref.shape[0] // sketch_rows):
        at = pl.ds(m * sketch_rows, sketch_rows)
        term = grad_ref[at, :] * sign_ref[at, :]
        total = term if total is None else total + term
    return total


def text_sketch(sel, parts, up_text, text_hidden_t, regrouped, signs, offsets, sketch_rows, name):
    rank, width = up_text.shape
    rep = LANES // rank
    text = text_hidden_t.shape[1]
    heads = width // LANES
    n_part = len(parts)
    down_rows = regrouped.shape[0]

    def kernel(sel_ref, *refs):
        tv_refs = refs[:n_part]
        up_ref, hid_ref, reg_ref, sign_ref, out_ref, grad_scr = refs[n_part:]
        grad_scr[...] = jnp.zeros_like(grad_scr)
        hidden = jnp.concatenate(split(hid_ref[...]), axis=0)
        back = jnp.zeros((text, LANES), jnp.float32)
        done = 0
        for tv_ref in tv_refs:

            def one(index, back, tv_ref=tv_ref, done=done):
                head = sel_ref[done + index]
                at = pl.multiple_of(head * LANES, LANES)
                up = jnp.concatenate([up_ref[:, pl.ds(at, LANES)]] * rep, axis=0)
                grad = jnp.zeros((3 * rank, LANES), jnp.float32)
                for tv in split(tv_ref[index]):
                    back += lax.dot_general(
                        tv, up, (((1,), (1,)), ((), ())), preferred_element_type=jnp.float32
                    )
                    grad += jnp.dot(hidden, tv, preferred_element_type=jnp.float32)
                grad = grad[:rank] + grad[rank : 2 * rank] + grad[2 * rank :]
                grad_scr[pl.ds(offsets[1] + head, rank, stride=heads), :] = grad
                return back

            back = lax.fori_loop(0, tv_ref.shape[0], one, back)
            done += tv_ref.shape[0]
        down = jnp.zeros((down_rows, LANES), jnp.float32)
        for piece in split(spread_rows(back, rep, rank)):
            down += jnp.dot(reg_ref[...], piece, preferred_element_type=jnp.float32)
        grad_scr[pl.ds(offsets[0], down_rows), :] = down
        out_ref[...] = signed_sum(grad_scr, sign_ref, sketch_rows)

    operands = [*parts, up_text, text_hidden_t, regrouped, signs]
    out_shape = (sketch_rows, LANES)
    return call(
        kernel,
        [(struct(out_shape, jnp.float32), whole(out_shape))],
        [whole(x.shape) for x in operands],
        (1,),
        [pltpu.VMEM(signs.shape, jnp.float32)],
        prefetch=1,
        name=name,
        flops=6 * text * down_rows * rep * LANES,
        nbytes=sum(x.size * x.dtype.itemsize for x in operands),
    )(sel, *operands)[0]


def finish(sel, pieces, up_image, hidden_t, regrouped, signs, text_part, offsets, sketch_scale, name):
    rank, width = up_image.shape
    rep = LANES // rank
    tokens = hidden_t.shape[1]
    heads = width // LANES
    half = heads // 2
    down_rows = regrouped.shape[0]
    flat = [(part, first, array) for part in (0, 1) for array, first in pieces[part]]
    n_piece = len(flat)
    sketch_rows = text_part.shape[0]

    def kernel(sel_ref, *refs):
        piece_refs = refs[:n_piece]
        up_ref, hid_ref, reg_ref, sign_ref, text_ref = refs[n_piece : n_piece + 5]
        value_ref, out_ref, grad_scr = refs[n_piece + 5 :]
        grad_scr[...] = jnp.zeros_like(grad_scr)
        for part in (0, 1):
            edges = sorted({first for p, first, _ in flat if p == part} | {half})
            for start, stop in zip(edges[:-1], edges[1:]):
                terms = [
                    (ref, first)
                    for (p, first, array), ref in zip(flat, piece_refs)
                    if p == part and first <= start < first + array.shape[0]
                ]

                def one(j, carry, terms=terms, part=part):
                    value = None
                    for ref, first in terms:
                        term = ref[j - first].astype(jnp.float32)
                        value = term if value is None else value + term
                    at = pl.multiple_of(sel_ref[part * half + j] * LANES, LANES)
                    value_ref[:, pl.ds(at, LANES)] = value.astype(jnp.bfloat16)
                    return carry

                lax.fori_loop(start, stop, one, 0)
        value = value_ref[...]
        up = jnp.concatenate([up_ref[...]] * rep, axis=0)
        back = lax.dot_general(
            value, up, (((1,), (1,)), ((), ())), preferred_element_type=jnp.float32
        )
        grad = jnp.dot(hid_ref[...], value, preferred_element_type=jnp.float32)
        for head in range(heads):
            grad_scr[pl.ds(offsets[1] + head, rank, stride=heads), :] = grad[
                :, head * LANES : (head + 1) * LANES
            ]
        back = back.astype(jnp.bfloat16).astype(jnp.float32)
        spread = spread_rows(back, rep, rank).astype(jnp.bfloat16)
        grad_scr[pl.ds(offsets[0], down_rows), :] = jnp.dot(
            reg_ref[...], spread, preferred_element_type=jnp.float32
        )
        total = signed_sum(grad_scr, sign_ref, sketch_rows) + text_ref[...]
        out_ref[...] = total * sketch_scale

    operands = [x for _, _, x in flat] + [up_image, hidden_t, regrouped, signs, text_part]
    outs = [
        (struct((tokens, width), jnp.bfloat16), whole((tokens, width))),
        (struct((sketch_rows, LANES), jnp.float32), whole((sketch_rows, LANES))),
    ]
    return call(
        kernel,
        outs,
        [whole(x.shape) for x in operands],
        (1,),
        [pltpu.VMEM(signs.shape, jnp.float32)],
        prefetch=1,
        name=name,
        flops=4 * tokens * down_rows * rep * LANES,
        nbytes=sum(x.size * x.dtype.itemsize for x in operands),
    )(sel, *operands)


def axis_sum(value, axis):
    count = lax.axis_size(axis)
    if count & (count - 1):
        return lax.psum(value, axis)
    stride = 1
    while stride < count:
        masks = [stride]
        if stride * 4 <= count:
            masks = [stride, 2 * stride, 3 * stride]
        received = [
            lax.ppermute(value, axis, [(i, i ^ mask) for i in range(count)]) for mask in masks
        ]
        value = value + received[0]
        if len(received) == 3:
            value = value + (received[1] + received[2])
        stride *= 2 * ((len(masks) + 1) // 2)
    return value


def per_device(
    clean_latents,
    gaussian_noise,
    text_states,
    queries,
    key_states,
    cotangent,
    text_keys,
    window_radii,
    timestep,
    sketch_seed,
    down_image,
    up_image,
    down_text,
    up_text,
):
    frame_count, row_count, col_count, value_width = queries.shape
    head_count = window_radii.shape[0]
    tokens = frame_count * row_count * col_count
    half = head_count // 2
    frames, rows = lax.axis_size("tm"), lax.axis_size("height")
    axes = ("tm", "height")
    score_scale = (value_width // head_count) ** (-0.5)
    frame_tile, row_tile = lax.axis_index("tm"), lax.axis_index("height")
    side = frame_tile % 2

    rank, model_width = up_image.shape[0], down_image.shape[0]
    down_rows, up_rows = rank * model_width // LANES, rank * value_width // LANES
    total_rows = 2 * (down_rows + up_rows)
    sketch_rows = SKETCH // LANES
    sketch_scale = (tokens * frames * rows * (total_rows // sketch_rows)) ** (-0.5)

    need = (window_radii[:, 1] > 0).astype(jnp.int32)
    ids = jnp.arange(head_count, dtype=jnp.int32)
    ahead = (need[None, :] > need[:, None]) | (
        (need[None, :] == need[:, None]) & (ids[None, :] < ids[:, None])
    )
    place = jnp.sum(ahead.astype(jnp.int32), axis=1)
    slot_ids = jnp.arange(half, dtype=jnp.int32)
    wanted = jnp.concatenate([2 * slot_ids + side, 2 * slot_ids + 1 - side])
    sel = jnp.sum(jnp.where(place[None, :] == wanted[:, None], ids[None, :], 0), axis=1)
    sel = sel.astype(jnp.int32)
    radii = window_radii.reshape(-1)

    def present(source, count, index):
        table = np.array([source(i, count) is not None for i in range(count)], np.int32)
        return jnp.sum(jnp.where(jnp.arange(count) == index, table, 0)).astype(jnp.int32)

    exist = jnp.stack(
        [
            present(even_partner, rows, row_tile),
            present(odd_partner, rows, row_tile),
            present(functools.partial(frame_source, "oself"), frames, frame_tile),
            present(functools.partial(frame_source, "osib"), frames, frame_tile),
        ]
    )

    all_slots = [
        (f, r) for r in ("own", "even", "odd") for f in ("self", "sib", "oself", "osib")
    ]
    pairs = {s: slot_pairs(s, frames, rows) for s in all_slots}
    all_slots = [s for s in all_slots if pairs[s]]
    own_slots = [s for s in all_slots if s[1] == "own"]
    row_slots = [s for s in all_slots if s[1] != "own"]
    outer_slots = [s for s in own_slots if s[0] in ("oself", "osib")]

    flat = lambda x: x.reshape(tokens, x.shape[-1])
    q2, k2, c2 = flat(queries), flat(key_states), flat(cotangent)
    level = timestep.astype(jnp.float32) / 1000.0

    def give_back(slot, array):
        return lax.ppermute(array, axes, [(b, a) for a, b in pairs[slot]])

    def branch(reach_rows):
        halo = {}
        if reach_rows:
            near = pack([k2], sel, reach_rows, "pack_keys")
            for slot in row_slots:
                halo[slot] = lax.ppermute(near[0 if is_mine(slot) else 1], axes, pairs[slot])
            order, _ = lax.optimization_barrier((sel, near[0]))
        else:
            order = sel
        mine, other = pack([q2, c2, k2], order, half, "pack_all")
        recv = lax.ppermute(other, axes, pairs[("sib", "own")])
        for slot in outer_slots:
            keys = (mine if is_mine(slot) else other)[2 * half :]
            halo[slot] = lax.ppermute(keys, axes, pairs[slot])
        regrouped, text_regrouped, hidden_t, text_hidden_t, signs = prepare(
            flat(clean_latents),
            flat(gaussian_noise),
            text_states,
            down_image.T,
            down_text.T,
            level,
            sketch_seed,
            total_rows,
            "prepare",
        )
        pieces = {0: [], 1: []}
        text_parts = []

        def attend(first, count, slots, after, name):
            order, _ = lax.optimization_barrier((sel, after))
            grads, text_value = attention(
                order, radii, exist, mine, recv, halo, text_keys, first, count, slots, half,
                score_scale, col_count, name,
            )
            text_parts.insert(0, text_value)
            for slot in slots:
                array = grads[slot]
                if slot != ("self", "own"):
                    array = give_back(slot, array)
                pieces[0 if is_mine(slot) else 1].append((array, first))

        if reach_rows < half:
            attend(reach_rows, half - reach_rows, own_slots, hidden_t, "attend_own")
        if reach_rows:
            after = text_parts[0] if text_parts else hidden_t
            attend(0, reach_rows, all_slots, after, "attend_rows")
        text_part = text_sketch(
            sel, text_parts, up_text, text_hidden_t, text_regrouped, signs,
            (down_rows + up_rows, 2 * down_rows + up_rows), sketch_rows, "text_sketch",
        )
        return finish(
            sel, pieces, up_image, hidden_t, regrouped, signs, text_part,
            (0, down_rows), sketch_scale, "finish",
        )

    branches = sorted({min(n, half) for n in BRANCHES} | {half})
    count = (jnp.sum(need) + 1) // 2
    index = jnp.sum((count > jnp.array(branches, jnp.int32)).astype(jnp.int32))
    value, sketch = lax.switch(index, [functools.partial(branch, n) for n in branches])
    sketch = axis_sum(axis_sum(sketch, "tm"), "height")
    return value.reshape(queries.shape), sketch.reshape(SKETCH)


def solution(mesh):
    tokens_spec = P("tm", "height", None, None)
    return jax.shard_map(
        per_device,
        mesh=mesh,
        in_specs=(
            tokens_spec,
            tokens_spec,
            P(),
            tokens_spec,
            tokens_spec,
            tokens_spec,
            P(),
            P(),
            P(),
            P(),
            P(),
            P(),
            P(),
            P(),
        ),
        out_specs=(tokens_spec, P()),
        check_vma=False,
    )
```
